32 devices in a mesh: section: 4 (over y, core), seq: 4 (over z), tp: 2 (over x).
Axes of the slice: x: 2, y: 2, z: 4, core: 2. Of those that a mesh axis runs over, the one named last changes fastest.
Arguments:
- queries: bfloat16 [768, 4096], P('seq', 'tp'), may hold values from -45 to 45
- keys: bfloat16 [64, 4096], P(('section', 'seq'), 'tp'), may hold values from -6 to 6
- values: bfloat16 [64, 4096], P(('section', 'seq'), 'tp'), may hold values from -6 to 6
- out_grad: bfloat16 [768, 4096], P('seq', 'tp'), may hold values from -48 to 48
- text_len: int32 [2], replicated, may hold values from 192 to 384, as said below
- key_len: int32 [4], replicated, may hold values from 8 to 16, as said below
Outputs:
- query_grad: bfloat16 [768, 4096], P('seq', 'tp')
- key_grad: float32 [64, 4096], P(('section', 'seq'), 'tp')
- value_grad: float32 [64, 4096], P(('section', 'seq'), 'tp')
The draws below stay inside these ranges and needn't reach their ends.
Inputs may be any that keep to these rules, and one draw needn't show every extreme that they name: `text_len`: one length per report sequence of 384 rows; rows at or past it are padding. `key_len`: live volume tokens of each slab of 16; the slab's later tokens are padding.
All inputs are finite; a program needn't handle non-finite values.
Results may differ from the reference program's by a relative error of at most 0.009.
Values may be sent and summed in bfloat16 or wider, within the bound.
A program may use at most 64 MiB of HBM per device.

```python
import math
import jax
import jax.numpy as jnp
from jax import lax

HEADS = 32
HD = 128
SEQS = 2
TEXT = 768
LENGTH = 384
KEYS = 16
SLABS = 4
VOL = 64


def drawn_pair(base):
    key_source = jax.random.fold_in(base, 11)
    query_source = jax.random.fold_in(base, 12)
    key_mat = jnp.clip(jax.random.normal(key_source, (VOL, HEADS * HD), jnp.float32), -6.0, 6.0)
    query_mat = jnp.clip(jax.random.normal(query_source, (TEXT, HEADS * HD), jnp.float32), -6.0, 6.0)
    return (query_mat, key_mat)


def draw_queries(key, part):
    return drawn_pair(key)[0].astype(jnp.bfloat16)


def draw_keys(key, part):
    return drawn_pair(key)[1].astype(jnp.bfloat16)


def ragged_lengths(key, count, most):
    halves = jax.random.split(key, 2)
    lengths = jax.random.randint(halves[0], (count,), most // 2, most)
    chosen = jax.random.randint(halves[1], (), 0, count)
    return jnp.where(jnp.arange(count) == chosen, most, lengths).astype(jnp.int32)


def draw_text_len(key, part):
    return ragged_lengths(key, SEQS, LENGTH)


def draw_key_len(key, part):
    return ragged_lengths(key, SLABS, KEYS)


def block_levels(key, dims, pieces, least, largest):
    gain = 1.0
    for axis_at, shards_of in pieces:
        heights = jax.random.uniform(jax.random.fold_in(jax.random.fold_in(key, 6), axis_at), (shards_of,), jnp.float32, least / len(pieces), largest / len(pieces))
        gain = gain * jnp.repeat(jnp.exp(heights), dims[axis_at] // shards_of).reshape((-1,) + (1,) * (len(dims) - 1 - axis_at))
    return gain


def gaussian(rng, dims, width, limit, cuts=(), kind=jnp.bfloat16):
    values = jax.random.normal(rng, dims, jnp.float32) * width
    if len(cuts) > 0:
        values = block_levels(rng, dims, cuts, -0.22, 0.18) * values
    return jnp.clip(values, min=-limit, max=limit).astype(kind)


def setup_inputs(seed: int = 0) -> dict:
    streams_of = jax.random.split(jax.random.key(seed), 7)
    return {
        "queries": draw_queries(jax.random.fold_in(streams_of[6], 71), 0),
        "keys": draw_keys(jax.random.fold_in(streams_of[6], 71), 0),
        "values": gaussian(streams_of[2], (VOL, HEADS * HD), 1.0, 6.0, ((0, 16), (1, 2))),
        "out_grad": gaussian(streams_of[3], (TEXT, HEADS * HD), 8.0, 48.0, ((0, 4), (1, 2))),
        "text_len": draw_text_len(jax.random.fold_in(streams_of[6], 71), 0),
        "key_len": draw_key_len(jax.random.fold_in(streams_of[6], 71), 0),
    }


def round_low(array):
    lowered = array.astype(jnp.bfloat16)
    lowered = lax.optimization_barrier(lowered)
    return lowered.astype(jnp.float32)

def reference(queries, keys, values, out_grad, text_len, key_len):
    score_scale = 1.0 / math.sqrt(HD)
    key_heads = keys.astype(jnp.float32).reshape(SLABS, KEYS, HEADS, HD)
    value_heads = values.astype(jnp.float32).reshape(SLABS, KEYS, HEADS, HD)
    key_live = jnp.arange(KEYS, dtype=jnp.int32)[None, :] < key_len[:, None]
    row_ids = jnp.arange(TEXT, dtype=jnp.int32)
    seq_ids = row_ids // LENGTH
    row_live = row_ids % LENGTH < text_len[seq_ids]
    masked_grad = jnp.where(row_live[:, None], out_grad, jnp.zeros_like(out_grad))
    block_rows = math.gcd(TEXT, 512)
    block_count = TEXT // block_rows
    query_blocks = queries.reshape(block_count, block_rows, HEADS, HD)
    grad_blocks = masked_grad.reshape(block_count, block_rows, HEADS, HD)

    def one_block(carry, inputs):
        key_acc, value_acc = carry
        query_block, grad_block = inputs
        query_full = query_block.astype(jnp.float32)
        grad_full = grad_block.astype(jnp.float32)
        scores = jnp.einsum('qhd,skhd->qhsk', query_full, key_heads) * score_scale
        scores = jnp.where(key_live[None, None], scores, jnp.float32(-1e+30))
        slab_max = lax.optimization_barrier(jnp.max(scores, axis=-1))
        expo = jnp.exp(scores - slab_max[..., None])
        slab_total = lax.optimization_barrier(jnp.sum(expo, axis=-1))
        slab_out = jnp.einsum('qhsk,skhd->qhsd', round_low(expo), value_heads)
        row_max = lax.optimization_barrier(jnp.max(slab_max, axis=-1))
        factor = jnp.exp(slab_max - row_max[..., None])
        total = lax.optimization_barrier(jnp.sum(slab_total * factor, axis=-1))
        attended = lax.optimization_barrier(jnp.sum(slab_out * factor[..., None], axis=2)) / total[..., None]
        row_dot = lax.optimization_barrier(jnp.sum(grad_full * attended, axis=-1))
        probs = jnp.exp(scores - row_max[..., None, None]) / total[..., None, None]
        probs_low = round_low(probs)
        prob_grad = jnp.einsum('qhd,skhd->qhsk', grad_full, value_heads)
        score_grad = round_low(probs * (prob_grad - row_dot[..., None, None]))
        slab_query = jnp.einsum('qhsk,skhd->sqhd', score_grad, key_heads) * score_scale
        query_grad = lax.optimization_barrier(jnp.sum(round_low(slab_query), axis=0)).astype(jnp.bfloat16)
        key_acc = key_acc + jnp.einsum('qhsk,qhd->skhd', score_grad, query_full) * score_scale
        value_acc = value_acc + jnp.einsum('qhsk,qhd->skhd', probs_low, grad_full)
        return ((key_acc, value_acc), query_grad)
    zeros_kv = jnp.zeros((SLABS, KEYS, HEADS, HD), jnp.float32)
    (key_acc, value_acc), query_grad = lax.scan(one_block, (zeros_kv, zeros_kv), (query_blocks, grad_blocks))
    return (query_grad.reshape(TEXT, HEADS * HD), key_acc.reshape(VOL, HEADS * HD), value_acc.reshape(VOL, HEADS * HD))
```

```python
import functools
import math

import jax
import jax.numpy as jnp
from jax import lax
from jax.experimental import pallas as pl
from jax.experimental.pallas import tpu as pltpu
from jax.sharding import PartitionSpec as P

HD = 128
SEQS = 2
MESH = pl.DeviceIdType.MESH


def each(low, high, step):
    if high - low <= 8:
        for k in range(low, high):
            step(k)
    else:
        lax.fori_loop(low, high, lambda k, c: (step(k), c)[1], 0)


def kernel(
    nsec, nseq,
    text_ref, klen_ref, q_hbm, k_ref, v_ref, g_hbm,
    qg_ref, kg_ref, vg_ref,
    q_ref, g_ref, gk, gv, kall, vall, full, part, inbox,
    local_sem, send1, recv1, send2, recv2, send3, recv3,
):
    sec = lax.axis_index("section")
    seq = lax.axis_index("seq")
    tok = k_ref.shape[0]
    rows, width = q_ref.shape
    heads = width // HD
    slab = nseq * tok
    vol = nsec * slab
    scale = 1.0 / math.sqrt(HD)

    local = [
        pltpu.make_async_copy(q_hbm, q_ref, local_sem.at[0]),
        pltpu.make_async_copy(g_hbm, g_ref, local_sem.at[1]),
        pltpu.make_async_copy(k_ref, gk.at[sec * nseq + seq], local_sem.at[2]),
        pltpu.make_async_copy(v_ref, gv.at[sec * nseq + seq], local_sem.at[3]),
    ]
    for copy in local:
        copy.start()

    barrier = pltpu.get_barrier_semaphore()

    def greet(axis, me, count):
        def one(k):
            pl.semaphore_signal(
                barrier, inc=1, device_id={axis: lax.rem(me + k, count)}, device_id_type=MESH
            )
        each(1, count, one)

    greet("seq", seq, nseq)
    greet("section", sec, nsec)
    pl.semaphore_wait(barrier, nseq + nsec - 2)

    def along_seq(k, which, src, dst):
        return pltpu.make_async_remote_copy(
            src_ref=src, dst_ref=dst.at[sec * nseq + seq],
            send_sem=send1.at[which, k], recv_sem=recv1.at[which, k],
            device_id={"seq": lax.rem(seq + k, nseq)}, device_id_type=MESH,
        )

    def along_section(k, p, which, src, dst):
        slot = sec * nseq + lax.rem(seq + nseq - k, nseq)
        return pltpu.make_async_remote_copy(
            src_ref=src, dst_ref=dst.at[slot],
            send_sem=send2.at[which, p, k], recv_sem=recv2.at[which, p, k],
            device_id={"section": lax.rem(sec + p, nsec)}, device_id_type=MESH,
        )

    pairs = ((0, k_ref, gk), (1, v_ref, gv))

    def start1(k):
        for which, src, dst in pairs:
            along_seq(k, which, src, dst).start()

    each(1, nseq, start1)
    for p in range(1, nsec):
        for which, src, dst in pairs:
            along_section(0, p, which, src, dst).start()

    def forward(k):
        slot = sec * nseq + lax.rem(seq + nseq - k, nseq)
        for which, src, dst in pairs:
            along_seq(k, which, src, dst).wait_recv()
            for p in range(1, nsec):
                along_section(k, p, which, dst.at[slot], dst).start()

    each(1, nseq, forward)

    def arrive(k):
        for which, src, dst in pairs:
            for p in range(1, nsec):
                along_section(k, p, which, src, dst).wait_recv()

    each(0, nseq, arrive)
    for copy in local:
        copy.wait()

    def spread(j):
        for src, dst in ((gk, kall), (gv, vall)):
            dst[j, 0:tok, :] = src[2 * j].astype(jnp.float32)
            dst[j, tok:2 * tok, :] = src[2 * j + 1].astype(jnp.float32)

    each(0, nsec * nseq // 2, spread)

    length = rows * nseq // SEQS
    position = seq * rows + lax.broadcasted_iota(jnp.int32, (1, rows), 1)
    alive = jnp.zeros((1, rows), jnp.int32)
    for s in range(SEQS):
        inside = (position >= s * length) & (position < s * length + text_ref[s])
        alive = jnp.where(inside, 1, alive)
    alive = alive > 0
    token = lax.broadcasted_iota(jnp.int32, (vol, rows), 0)
    limit = jnp.zeros((vol, rows), jnp.int32)
    for s in range(nsec):
        limit = jnp.where(token >= s * slab, s * slab + klen_ref[s], limit)
    live = token < limit

    def head(h):
        cols = pl.ds(pl.multiple_of(h * HD, HD), HD)
        q = q_ref[:, cols]
        g = g_ref[:, cols]
        key = kall[:, :, cols].reshape(vol, HD).astype(jnp.bfloat16)
        value = vall[:, :, cols].reshape(vol, HD).astype(jnp.bfloat16)
        nt = (((1,), (1,)), ((), ()))
        scores = lax.dot_general(key, q, nt, preferred_element_type=jnp.float32) * scale
        prob_grad = lax.dot_general(value, g, nt, preferred_element_type=jnp.float32)
        scores = jnp.where(live, scores, jnp.float32(-1e30))
        expo = jnp.exp(scores - jnp.max(scores, axis=0, keepdims=True))
        total = jnp.sum(expo, axis=0, keepdims=True)
        probs = expo * jnp.where(alive, 1.0 / total, 0.0)
        row_dot = jnp.sum(probs * prob_grad, axis=0, keepdims=True)
        score_grad = (probs * (prob_grad - row_dot)).astype(jnp.bfloat16)
        tn = (((0,), (0,)), ((), ()))
        qg = lax.dot_general(score_grad, key, tn, preferred_element_type=jnp.float32) * scale
        qg_ref[:, cols] = qg.astype(jnp.bfloat16)
        nn = (((1,), (0,)), ((), ()))
        full[0, :, cols] = (
            lax.dot_general(score_grad, q, nn, preferred_element_type=jnp.float32) * scale
        )
        full[1, :, cols] = lax.dot_general(
            probs.astype(jnp.bfloat16), g, nn, preferred_element_type=jnp.float32
        )

    unroll = 4 if heads % 4 == 0 and vol <= 128 else 1

    def several(i, c):
        for u in range(unroll):
            head(i * unroll + u)
        return c

    lax.fori_loop(0, heads // unroll, several, 0)

    def gather_rows(j):
        at = pl.multiple_of(sec * slab + j * 2 * tok, 2 * tok)
        for which in range(2):
            both = full[which, pl.ds(at, 2 * tok), :]
            part[2 * j, which] = both[0:tok]
            part[2 * j + 1, which] = both[tok:2 * tok]

    each(0, nseq // 2, gather_rows)

    def share(k):
        dest = lax.rem(seq + k, nseq)
        return pltpu.make_async_remote_copy(
            src_ref=part.at[dest], dst_ref=inbox.at[k],
            send_sem=send3.at[k], recv_sem=recv3.at[k],
            device_id={"seq": dest}, device_id_type=MESH,
        )

    each(1, nseq, lambda k: share(k).start())
    kg_ref[...] = part[seq, 0]
    vg_ref[...] = part[seq, 1]

    def add(k):
        share(k).wait_recv()
        kg_ref[...] += inbox[k, 0]
        vg_ref[...] += inbox[k, 1]

    each(1, nseq, add)

    def drain(k):
        share(k).wait_send()
        for which, src, dst in pairs:
            along_seq(k, which, src, dst).wait_send()

    each(1, nseq, drain)

    def drain2(k):
        for which, src, dst in pairs:
            for p in range(1, nsec):
                along_section(k, p, which, src, dst).wait_send()

    each(0, nseq, drain2)


def solution(mesh):
    nsec, nseq = mesh.shape["section"], mesh.shape["seq"]

    def per_device(queries, keys, values, out_grad, text_len, key_len):
        rows, width = queries.shape
        tok = keys.shape[0]
        slots = nsec * nseq
        vmem = pl.BlockSpec(memory_space=pltpu.VMEM)
        smem = pl.BlockSpec(memory_space=pltpu.SMEM)
        hbm = pl.BlockSpec(memory_space=pl.ANY)
        dma = pltpu.SemaphoreType.DMA
        return pl.pallas_call(
            functools.partial(kernel, nsec, nseq),
            out_shape=(
                jax.ShapeDtypeStruct((rows, width), jnp.bfloat16),
                jax.ShapeDtypeStruct((tok, width), jnp.float32),
                jax.ShapeDtypeStruct((tok, width), jnp.float32),
            ),
            in_specs=[smem, smem, hbm, vmem, vmem, hbm],
            out_specs=(vmem, vmem, vmem),
            scratch_shapes=[
                pltpu.VMEM((rows, width), jnp.bfloat16),
                pltpu.VMEM((rows, width), jnp.bfloat16),
                pltpu.VMEM((slots, tok, width), jnp.bfloat16),
                pltpu.VMEM((slots, tok, width), jnp.bfloat16),
                pltpu.VMEM((slots // 2, 2 * tok, width), jnp.float32),
                pltpu.VMEM((slots // 2, 2 * tok, width), jnp.float32),
                pltpu.VMEM((2, slots * tok, width), jnp.float32),
                pltpu.VMEM((nseq, 2, tok, width), jnp.float32),
                pltpu.VMEM((nseq, 2, tok, width), jnp.float32),
                dma((4,)),
                dma((2, nseq)), dma((2, nseq)),
                dma((2, nsec, nseq)), dma((2, nsec, nseq)),
                dma((nseq,)), dma((nseq,)),
            ],
            compiler_params=pltpu.CompilerParams(
                collective_id=0, has_side_effects=True, vmem_limit_bytes=64000 * 1024
            ),
        )(text_len, key_len, queries, keys, values, out_grad)

    in_specs = (
        P("seq", "tp"),
        P(("section", "seq"), "tp"),
        P(("section", "seq"), "tp"),
        P("seq", "tp"),
        P(),
        P(),
    )
    out_specs = (P("seq", "tp"), P(("section", "seq"), "tp"), P(("section", "seq"), "tp"))
    return jax.shard_map(
        per_device, mesh=mesh, in_specs=in_specs, out_specs=out_specs, check_vma=False
    )
```

```python
import functools
import math

import jax
import jax.numpy as jnp
from jax import lax
from jax.experimental import pallas as pl
from jax.experimental.pallas import tpu as pltpu
from jax.sharding import PartitionSpec as P

HD = 128
SEQS = 2
MESH = pl.DeviceIdType.MESH


def each(low, high, step):
    if high - low <= 8:
        for k in range(low, high):
            step(k)
    else:
        lax.fori_loop(low, high, lambda k, c: (step(k), c)[1], 0)


def kernel(
    nsec, nseq,
    text_ref, klen_ref, q_hbm, k_ref, v_ref, g_hbm,
    qg_ref, kg_ref, vg_ref,
    q_ref, g_ref, gk, gv, kall, vall, full, mine, part, inbox,
    local_sem, send1, recv1, send2, recv2, send3, recv3,
):
    sec = lax.axis_index("section")
    seq = lax.axis_index("seq")
    tok = k_ref.shape[0]
    rows, width = q_ref.shape
    heads = width // HD
    slab = nseq * tok
    vol = nsec * slab
    scale = 1.0 / math.sqrt(HD)

    local = [
        pltpu.make_async_copy(q_hbm, q_ref, local_sem.at[0]),
        pltpu.make_async_copy(g_hbm, g_ref, local_sem.at[1]),
        pltpu.make_async_copy(k_ref, gk.at[sec * nseq + seq], local_sem.at[2]),
        pltpu.make_async_copy(v_ref, gv.at[sec * nseq + seq], local_sem.at[3]),
    ]
    for copy in local:
        copy.start()

    barrier = pltpu.get_barrier_semaphore()

    def greet(axis, me, count):
        def one(k):
            pl.semaphore_signal(
                barrier, inc=1, device_id={axis: lax.rem(me + k, count)}, device_id_type=MESH
            )
        each(1, count, one)

    greet("seq", seq, nseq)
    greet("section", sec, nsec)
    pl.semaphore_wait(barrier, nseq + nsec - 2)

    def along_seq(k, which, src, dst):
        return pltpu.make_async_remote_copy(
            src_ref=src, dst_ref=dst.at[sec * nseq + seq],
            send_sem=send1.at[which, k], recv_sem=recv1.at[which, k],
            device_id={"seq": lax.rem(seq + k, nseq)}, device_id_type=MESH,
        )

    twin = sec + 1 - 2 * lax.rem(sec, 2)
    across = lax.rem(sec + 2, 4)

    def slot_of(owner, k):
        return owner * nseq + lax.rem(seq + nseq - k, nseq)

    def along_section(k, p, which, src, dst):
        owner = across if p == 2 else sec
        return pltpu.make_async_remote_copy(
            src_ref=src, dst_ref=dst.at[slot_of(owner, k)],
            send_sem=send2.at[which, p, k], recv_sem=recv2.at[which, p, k],
            device_id={"section": across if p == 0 else twin}, device_id_type=MESH,
        )

    pairs = ((0, k_ref, gk), (1, v_ref, gv))

    def start1(k):
        for which, src, dst in pairs:
            along_seq(k, which, src, dst).start()

    each(1, nseq, start1)
    for p in range(2):
        for which, src, dst in pairs:
            along_section(0, p, which, src, dst).start()

    def relay(k):
        for which, src, dst in pairs:
            along_section(k, 0, which, src, dst).wait_recv()
            along_section(k, 2, which, dst.at[slot_of(across, k)], dst).start()

    def forward(k):
        for which, src, dst in pairs:
            along_seq(k, which, src, dst).wait_recv()
            for p in range(2):
                along_section(k, p, which, dst.at[slot_of(sec, k)], dst).start()
        relay(k - 1)

    each(1, nseq, forward)
    relay(nseq - 1)

    def arrive(k):
        for which, src, dst in pairs:
            for p in range(1, 3):
                along_section(k, p, which, src, dst).wait_recv()

    each(0, nseq, arrive)
    for copy in local:
        copy.wait()

    def spread(j):
        for src, dst in ((gk, kall), (gv, vall)):
            dst[j, 0:tok, :] = src[2 * j].astype(jnp.float32)
            dst[j, tok:2 * tok, :] = src[2 * j + 1].astype(jnp.float32)

    each(0, nsec * nseq // 2, spread)

    length = rows * nseq // SEQS
    position = seq * rows + lax.broadcasted_iota(jnp.int32, (1, rows), 1)
    alive = jnp.zeros((1, rows), jnp.int32)
    for s in range(SEQS):
        inside = (position >= s * length) & (position < s * length + text_ref[s])
        alive = jnp.where(inside, 1, alive)
    alive = alive > 0
    token = lax.broadcasted_iota(jnp.int32, (vol, rows), 0)
    limit = jnp.zeros((vol, rows), jnp.int32)
    for s in range(nsec):
        limit = jnp.where(token >= s * slab, s * slab + klen_ref[s], limit)
    live = token < limit

    def head(h):
        cols = pl.ds(pl.multiple_of(h * HD, HD), HD)
        q = q_ref[:, cols]
        g = g_ref[:, cols]
        key = kall[:, :, cols].reshape(vol, HD).astype(jnp.bfloat16)
        value = vall[:, :, cols].reshape(vol, HD).astype(jnp.bfloat16)
        nt = (((1,), (1,)), ((), ()))
        scores = lax.dot_general(key, q, nt, preferred_element_type=jnp.float32) * scale
        prob_grad = lax.dot_general(value, g, nt, preferred_element_type=jnp.float32)
        scores = jnp.where(live, scores, jnp.float32(-1e30))
        expo = jnp.exp(scores - jnp.max(scores, axis=0, keepdims=True))
        total = jnp.sum(expo, axis=0, keepdims=True)
        probs = expo * jnp.where(alive, 1.0 / total, 0.0)
        row_dot = jnp.sum(probs * prob_grad, axis=0, keepdims=True)
        score_grad = (probs * (prob_grad - row_dot)).astype(jnp.bfloat16)
        tn = (((0,), (0,)), ((), ()))
        qg = lax.dot_general(score_grad, key, tn, preferred_element_type=jnp.float32) * scale
        qg_ref[:, cols] = qg.astype(jnp.bfloat16)
        nn = (((1,), (0,)), ((), ()))
        full[0, :, cols] = (
            lax.dot_general(score_grad, q, nn, preferred_element_type=jnp.float32) * scale
        )
        full[1, :, cols] = lax.dot_general(
            probs.astype(jnp.bfloat16), g, nn, preferred_element_type=jnp.float32
        )

    groups = 4
    per_group = heads // groups
    span = width // groups

    def share(k, group):
        dest = lax.rem(seq + k, nseq)
        cols = pl.ds(group * span, span)
        return pltpu.make_async_remote_copy(
            src_ref=part.at[dest, :, :, cols], dst_ref=inbox.at[k, :, :, cols],
            send_sem=send3.at[group, k], recv_sem=recv3.at[group, k],
            device_id={"seq": dest}, device_id_type=MESH,
        )

    for group in range(groups):
        if vol <= 128:
            for u in range(per_group):
                head(group * per_group + u)
        else:
            lax.fori_loop(0, per_group, lambda u, c: (head(group * per_group + u), c)[1], 0)
        cols = pl.ds(group * span, span)

        def gather_rows(j):
            at = pl.multiple_of(sec * slab + j * 2 * tok, 2 * tok)
            for which in range(2):
                both = full[which, pl.ds(at, 2 * tok), cols]
                for half in range(2):
                    piece = both[half * tok:(half + 1) * tok]
                    mine[2 * j + half, which, :, cols] = piece
                    part[2 * j + half, which, :, cols] = piece.astype(jnp.bfloat16)

        each(0, nseq // 2, gather_rows)
        if group > 0:
            each(1, nseq, lambda k: share(k, group - 1).start())
    kg_ref[...] = mine[seq, 0]
    vg_ref[...] = mine[seq, 1]
    each(1, nseq, lambda k: share(k, groups - 1).start())

    def add(k):
        for group in range(groups):
            share(k, group).wait_recv()
        kg_ref[...] += inbox[k, 0].astype(jnp.float32)
        vg_ref[...] += inbox[k, 1].astype(jnp.float32)

    each(1, nseq, add)

    def drain(k):
        for group in range(groups):
            share(k, group).wait_send()
        for which, src, dst in pairs:
            along_seq(k, which, src, dst).wait_send()

    each(1, nseq, drain)

    def drain2(k):
        for which, src, dst in pairs:
            for p in range(3):
                along_section(k, p, which, src, dst).wait_send()

    each(0, nseq, drain2)


def solution(mesh):
    nsec, nseq = mesh.shape["section"], mesh.shape["seq"]

    def per_device(queries, keys, values, out_grad, text_len, key_len):
        rows, width = queries.shape
        tok = keys.shape[0]
        slots = nsec * nseq
        vmem = pl.BlockSpec(memory_space=pltpu.VMEM)
        smem = pl.BlockSpec(memory_space=pltpu.SMEM)
        hbm = pl.BlockSpec(memory_space=pl.ANY)
        dma = pltpu.SemaphoreType.DMA
        return pl.pallas_call(
            functools.partial(kernel, nsec, nseq),
            out_shape=(
                jax.ShapeDtypeStruct((rows, width), jnp.bfloat16),
                jax.ShapeDtypeStruct((tok, width), jnp.float32),
                jax.ShapeDtypeStruct((tok, width), jnp.float32),
            ),
            in_specs=[smem, smem, hbm, vmem, vmem, hbm],
            out_specs=(vmem, vmem, vmem),
            scratch_shapes=[
                pltpu.VMEM((rows, width), jnp.bfloat16),
                pltpu.VMEM((rows, width), jnp.bfloat16),
                pltpu.VMEM((slots, tok, width), jnp.bfloat16),
                pltpu.VMEM((slots, tok, width), jnp.bfloat16),
                pltpu.VMEM((slots // 2, 2 * tok, width), jnp.float32),
                pltpu.VMEM((slots // 2, 2 * tok, width), jnp.float32),
                pltpu.VMEM((2, slots * tok, width), jnp.float32),
                pltpu.VMEM((nseq, 2, tok, width), jnp.float32),
                pltpu.VMEM((nseq, 2, tok, width), jnp.bfloat16),
                pltpu.VMEM((nseq, 2, tok, width), jnp.bfloat16),
                dma((4,)),
                dma((2, nseq)), dma((2, nseq)),
                dma((2, nsec, nseq)), dma((2, nsec, nseq)),
                dma((4, nseq)), dma((4, nseq)),
            ],
            compiler_params=pltpu.CompilerParams(
                collective_id=0, has_side_effects=True, vmem_limit_bytes=64000 * 1024
            ),
        )(text_len, key_len, queries, keys, values, out_grad)

    in_specs = (
        P("seq", "tp"),
        P(("section", "seq"), "tp"),
        P(("section", "seq"), "tp"),
        P("seq", "tp"),
        P(),
        P(),
    )
    out_specs = (P("seq", "tp"), P(("section", "seq"), "tp"), P(("section", "seq"), "tp"))
    return jax.shard_map(
        per_device, mesh=mesh, in_specs=in_specs, out_specs=out_specs, check_vma=False
    )
```
